32 devices in a mesh: comp: 16 (over z, x, core), lev: 2 (over y).
Axes of the slice: x: 2, y: 2, z: 4, core: 2. Of those that a mesh axis runs over, the one named last changes fastest.
Arguments:
- atm_temp: float32 [72, 4096], P('lev', 'comp'), may hold values from 0.7 to 1.3
- atm_vapor: float32 [72, 4096], P('lev', 'comp'), may hold values from 0.05 to 2
- span_dest: int32 [4096], P('comp'), may hold values from 0 to 15, as said below
- kabs: float32 [128, 72], replicated, may hold values from 0.01 to 4
- pfrac: float32 [128], replicated, may hold values from 0.5 to 2
- ocean_owner: int32 [4096], P(('comp', 'lev')), may hold values from 0 to 15, as said below
- remap_idx: int32 [4, 128, 256], P(None, 'comp', 'lev'), may hold values from 0 to 127
- remap_w: float32 [4, 128, 256], P(None, 'comp', 'lev'), may hold values from 0.05 to 0.45
- near_ground_gust_magnitude: float32 [128, 256], P('comp', 'lev'), may hold values from 0.3 to 3
- ocean_state: float32 [2, 80, 128, 256], P(None, None, 'comp', 'lev'), may hold values from -1.2 to 1.2
- gather_source_positions: int32 [4, 4096], P(None, ('comp', 'lev')), may hold values from 0 to 1023
- gather_source_shares: float32 [4, 4096], P(None, ('comp', 'lev')), may hold values from 0.05 to 0.45
Outputs:
- radiative_warming: float32 [72, 4096], P(None, ('comp', 'lev'))
- marine_anomalies_after: float32 [2, 80, 128, 256], P(None, None, 'comp', 'lev')
- parameterized_skin_warmth: float32 [4096], P(('comp', 'lev'))
The draws below stay inside these ranges and needn't reach their ends.
Inputs may be any that keep to these rules, and one draw needn't show every extreme that they name: `span_dest`: in each aligned block of 256 entries every value appears exactly 16 times. `ocean_owner`: in each aligned block of 128 entries every value appears exactly 8 times.
All inputs are finite; a program needn't handle non-finite values.
Results may differ from the reference program's by a relative error of at most 0.0001.
Values sent between devices are 32-bit elements; how exact they have to be, the bound alone decides.
No kernel may reach another device: no remote copies, remote signals or barrier semaphores. Data moves between devices by JAX's collectives and lax.ppermute only.
A program may use at most 64 MiB of HBM per device.

```python
import math
import jax
import jax.numpy as jnp
from jax import lax

LEVA = 72
LEVO = 80
GPTS = 128
TAPS = 4
NSTEP = 4
PROFILES_PER_RUN = 128
OYD = 8
OXD = 128
TILE_TOTAL = 16
RUNS_PER_TILE = 2
COL_DEV = 256
PROFILE_TOTAL = 4096
CAP = 16
PROFILES_PER_STRIP = 8
OY = 128
OX = 256


def spread_blocks(block_key, blocks, width, groups):
    block_keys = jax.random.split(block_key, blocks)
    pattern = jnp.arange(width, dtype=jnp.int32) % groups
    shuffled = jax.vmap(lambda sub_key: jax.random.permutation(sub_key, pattern))(block_keys)
    return shuffled.reshape(blocks * width)


def draw_span_dest(key, part):
    return spread_blocks(jax.random.fold_in(key, 11), PROFILE_TOTAL // COL_DEV, COL_DEV, PROFILE_TOTAL // COL_DEV)


def draw_ocean_owner(key, part):
    return spread_blocks(jax.random.fold_in(key, 23), PROFILE_TOTAL // PROFILES_PER_RUN, PROFILES_PER_RUN, PROFILE_TOTAL // COL_DEV)


def place_ends(result, stream_key, least, largest):
    longest = result.shape.index(max(result.shape))
    spots = []
    for shift in (0, 1):
        where = [jax.random.randint(jax.random.fold_in(stream_key, axis), (), 0, length) for axis, length in enumerate(result.shape)]
        where[longest] = (where[longest] + shift) % result.shape[longest]
        spots.append(tuple(where))
    return result.at[spots[0]].set(least).at[spots[1]].set(largest)


def steps_of(own_key, extent, cuts, low, high):
    level = 1.0
    for axis_at, blocks in cuts:
        steps = jax.random.uniform(jax.random.fold_in(jax.random.fold_in(own_key, 6), axis_at), (blocks,), jnp.float32, low / len(cuts), high / len(cuts))
        level = level * jnp.repeat(jnp.exp(steps), extent[axis_at] // blocks).reshape((-1,) + (1,) * (len(extent) - 1 - axis_at))
    return level


def normal_values(stream_key, shape, scale, bound, cuts=(), kind=jnp.bfloat16):
    result = jax.random.normal(stream_key, shape, jnp.float32) * scale
    if len(cuts) > 0:
        result = steps_of(stream_key, shape, cuts, -0.22, 0.18) * result
    return jnp.clip(result, min=-bound, max=bound).astype(kind)


def setup_inputs(seed: int = 0) -> dict:
    key_of = jax.random.split(jax.random.key(seed), 13)
    return {
        "atm_temp": jnp.clip(0.7 + 0.59999996 * jax.random.uniform(key_of[0], (LEVA, PROFILE_TOTAL), jnp.float32) ** steps_of(key_of[0], (LEVA, PROFILE_TOTAL), ((0, 2), (1, 16)), -0.2, 0.2), 0.7, 1.3),
        "atm_vapor": jnp.clip(jnp.exp(math.log(2.0) - 3.6888794 * jax.random.uniform(key_of[1], (LEVA, PROFILE_TOTAL), jnp.float32) ** steps_of(key_of[1], (LEVA, PROFILE_TOTAL), ((0, 2), (1, 16)), -0.2, 0.2)), 0.05, 2.0),
        "span_dest": draw_span_dest(jax.random.fold_in(key_of[12], 71), 0),
        "kabs": jnp.clip(jnp.exp(jax.random.uniform(key_of[3], (GPTS, LEVA), jnp.float32, math.log(0.01), math.log(4.0))), 0.01, 4.0),
        "pfrac": jnp.clip(jnp.exp(jax.random.uniform(key_of[4], (GPTS,), jnp.float32, math.log(0.5), math.log(2.0))), 0.5, 2.0),
        "ocean_owner": draw_ocean_owner(jax.random.fold_in(key_of[12], 71), 0),
        "remap_idx": place_ends(jax.random.randint(key_of[6], (TAPS, OY, OX), 0, PROFILES_PER_RUN), jax.random.fold_in(key_of[6], 1), 0, PROFILES_PER_RUN - 1).astype(jnp.int32),
        "remap_w": jnp.clip(0.05 + 0.39999999 * jax.random.uniform(key_of[7], (TAPS, OY, OX), jnp.float32) ** steps_of(key_of[7], (TAPS, OY, OX), ((1, 16), (2, 2)), -0.2, 0.2), 0.05, 0.45),
        "near_ground_gust_magnitude": jnp.clip(jnp.exp(math.log(3.0) - 2.3025851 * jax.random.uniform(key_of[8], (OY, OX), jnp.float32) ** steps_of(key_of[8], (OY, OX), ((0, 16), (1, 2)), -0.2, 0.2)), 0.3, 3.0),
        "ocean_state": normal_values(key_of[9], (2, LEVO, OY, OX), 0.2, 1.2, ((2, 16), (3, 2)), jnp.float32),
        "gather_source_positions": place_ends(jax.random.randint(key_of[10], (TAPS, PROFILE_TOTAL), 0, OYD * OXD), jax.random.fold_in(key_of[10], 1), 0, (OYD * OXD) - 1).astype(jnp.int32),
        "gather_source_shares": jnp.clip(0.05 + 0.39999999 * jax.random.uniform(key_of[11], (TAPS, PROFILE_TOTAL), jnp.float32) ** steps_of(key_of[11], (TAPS, PROFILE_TOTAL), ((1, 32),), -0.2, 0.2), 0.05, 0.45),
    }


diffusion_rate = 0.24
baseline_skin_warmth = 1.0
reference_salt = 1.0
skin_radiative_efficiency = 0.7
thermal_coupling_coefficient = 0.6
clausius_magnitude = 0.8
clausius_gradient = 1.5
evap_coef = 0.6
thermal_increment = 0.5
salt_step = 0.5


def compose(earlier, latter):
    return (earlier[0] * latter[0], latter[0] * earlier[1] + latter[1])


def radiate(temp_cols, vapor_cols, kabs, pfrac):
    levels = temp_cols.shape[0]
    columns = temp_cols.shape[1]
    points = kabs.shape[0]
    block_size = math.gcd(32, points)
    kabs_blocks = kabs.reshape(points // block_size, block_size, levels)
    pfrac_blocks = pfrac.reshape(points // block_size, block_size)
    planck = temp_cols ** 4

    def one_block(running, pieces):
        kabs_piece, pfrac_piece = pieces
        transmit = jnp.exp(-kabs_piece[:, :, None] * vapor_cols[None, :, :])
        source = pfrac_piece[:, None, None] * planck[None, :, :]
        emitted = (1.0 - transmit) * source
        downward = lax.associative_scan(compose, (transmit, emitted), axis=1)[1]
        through, risen = lax.associative_scan(compose, (transmit, emitted), reverse=True, axis=1)
        ground = source[:, levels - 1, :]
        upward = through * ground[:, None, :] + risen
        top_zero = jnp.zeros((block_size, 1, columns), jnp.float32)
        up_full = jnp.concatenate([upward, ground[:, None, :]], axis=1)
        down_full = jnp.concatenate([top_zero, downward], axis=1)
        net_sum = running[0] + jnp.sum(up_full - down_full, axis=0)
        ground_down = running[1] + jnp.sum(downward[:, levels - 1, :], axis=0)
        return (net_sum, ground_down), None

    start = (jnp.zeros((levels + 1, columns), jnp.float32), jnp.zeros((columns,), jnp.float32))
    (net_sum, ground_down), unused = lax.scan(one_block, start, (kabs_blocks, pfrac_blocks))
    net_mean = net_sum / points
    return net_mean[1:] - net_mean[:-1], ground_down / points


def stencil(padded):
    inner = padded[..., 1:-1, 1:-1]
    beside_all = (padded[..., :-2, 1:-1] + padded[..., 2:, 1:-1]) + (padded[..., 1:-1, :-2] + padded[..., 1:-1, 2:])
    return inner + diffusion_rate * (beside_all - 4.0 * inner)


def diffuse_slice(layer):
    for repeat in range(NSTEP):
        layer = stencil(jnp.pad(layer, 1))
    return layer


def skin_increment(smoothed_tracer, marine_tracer_stack, near_ground_gust_magnitude):
    topmost_theta_anomaly = smoothed_tracer[0, 0]
    salt_top = smoothed_tracer[1, 0]
    present_skin_warmth = baseline_skin_warmth + topmost_theta_anomaly
    skin_thermal_transfer = marine_tracer_stack[0] - skin_radiative_efficiency * present_skin_warmth ** 4 + thermal_coupling_coefficient * near_ground_gust_magnitude * (marine_tracer_stack[1] - present_skin_warmth)
    clausius_humidity = clausius_magnitude * jnp.exp(clausius_gradient * (present_skin_warmth - baseline_skin_warmth))
    evaporation = evap_coef * near_ground_gust_magnitude * (clausius_humidity - marine_tracer_stack[2])
    revised_theta_anomaly = topmost_theta_anomaly + thermal_increment * skin_thermal_transfer
    revised_salinity_anomaly = salt_top + salt_step * (reference_salt + salt_top) * evaporation
    return smoothed_tracer.at[0, 0].set(revised_theta_anomaly).at[1, 0].set(revised_salinity_anomaly), revised_theta_anomaly


def reference(atm_temp, atm_vapor, span_dest, kabs, pfrac, ocean_owner, remap_idx, remap_w, near_ground_gust_magnitude, ocean_state, gather_source_positions, gather_source_shares):
    dest_sorted = jnp.argsort(span_dest.reshape(TILE_TOTAL, COL_DEV), axis=1, stable=True).astype(jnp.int32)
    column_ids = dest_sorted + (jnp.arange(TILE_TOTAL, dtype=jnp.int32) * COL_DEV)[:, None]
    physics_order = column_ids.reshape(TILE_TOTAL, TILE_TOTAL, CAP).transpose(1, 0, 2).reshape(PROFILE_TOTAL)
    temp_phys = jnp.take(atm_temp, physics_order, axis=1)
    vapor_phys = jnp.take(atm_vapor, physics_order, axis=1)
    temp_groups = temp_phys.reshape(LEVA, TILE_TOTAL, COL_DEV).transpose(1, 0, 2)
    vapor_groups = vapor_phys.reshape(LEVA, TILE_TOTAL, COL_DEV).transpose(1, 0, 2)
    heat_groups, down_groups = lax.map(lambda pieces: radiate(pieces[0], pieces[1], kabs, pfrac), (temp_groups, vapor_groups))
    radiative_warming = heat_groups.transpose(1, 0, 2).reshape(LEVA, PROFILE_TOTAL)
    down_surface = down_groups.reshape(PROFILE_TOTAL)
    surface = jnp.stack([down_surface, temp_phys[LEVA - 1], vapor_phys[LEVA - 1]])
    owner_ordering = jnp.argsort(ocean_owner.reshape(TILE_TOTAL, RUNS_PER_TILE, PROFILES_PER_RUN), axis=2, stable=True).astype(jnp.int32)
    sorted_surface = jnp.take_along_axis(surface.reshape(3, TILE_TOTAL, RUNS_PER_TILE, PROFILES_PER_RUN), owner_ordering[None], axis=3)
    intake = sorted_surface.reshape(3, TILE_TOTAL, RUNS_PER_TILE, TILE_TOTAL, PROFILES_PER_STRIP).transpose(0, 3, 2, 1, 4).reshape(3, PROFILE_TOTAL)
    row_band = jnp.arange(OY, dtype=jnp.int32) // OYD
    col_band = jnp.arange(OX, dtype=jnp.int32) // OXD
    block_start = (row_band[:, None] * RUNS_PER_TILE + col_band[None, :]) * PROFILES_PER_RUN
    flat_index = (block_start[None] + remap_idx).reshape(-1)
    gathered = jnp.take(intake, flat_index, axis=1).reshape(3, TAPS, OY, OX)
    marine_tracer_stack = jnp.sum(remap_w[None] * gathered, axis=1)
    layers = lax.map(diffuse_slice, ocean_state.reshape(2 * LEVO, OY, OX))
    smoothed_tracer = layers.reshape(2, LEVO, OY, OX)
    marine_anomalies_after, revised_theta_anomaly = skin_increment(smoothed_tracer, marine_tracer_stack, near_ground_gust_magnitude)
    revised_skin_warmth = baseline_skin_warmth + revised_theta_anomaly
    slot_block = jnp.arange(PROFILE_TOTAL, dtype=jnp.int32) // PROFILES_PER_RUN
    band_of = slot_block // RUNS_PER_TILE
    batch_of = slot_block % RUNS_PER_TILE
    worldwide_ordinate = band_of[None] * OYD + gather_source_positions // OXD
    worldwide_abscissa = batch_of[None] * OXD + gather_source_positions % OXD
    placed_skin_warmth = jnp.sum(gather_source_shares * revised_skin_warmth[worldwide_ordinate, worldwide_abscissa], axis=0)
    sorted_skin_warmth = placed_skin_warmth.reshape(TILE_TOTAL, RUNS_PER_TILE, TILE_TOTAL, PROFILES_PER_STRIP).transpose(2, 1, 0, 3).reshape(TILE_TOTAL, RUNS_PER_TILE, PROFILES_PER_RUN)
    undo_reorder_map = jnp.argsort(owner_ordering, axis=2).astype(jnp.int32)
    parameterized_skin_warmth = jnp.take_along_axis(sorted_skin_warmth, undo_reorder_map, axis=2).reshape(PROFILE_TOTAL)
    return radiative_warming, marine_anomalies_after, parameterized_skin_warmth
```

```python
import math

import jax
import jax.numpy as jnp
from jax import lax
from jax.experimental import pallas as pl
from jax.experimental.pallas import tpu as pltpu
from jax.sharding import PartitionSpec as P

NSTEP = 4
LANES = 128
SUB = 8
CAP = 16
STRIP = 4
SLOTS = LANES // STRIP

diffusion_rate = 0.24
skin_radiative_efficiency = 0.7
thermal_coupling_coefficient = 0.6
clausius_magnitude = 0.8
clausius_gradient = 1.5
evap_coef = 0.6
thermal_increment = 0.5
salt_step = 0.5

VMEM = pl.BlockSpec(memory_space=pltpu.VMEM)


def iota(shape, dim):
    return lax.broadcasted_iota(jnp.int32, shape, dim)


def lane_roll(x, shift):
    if isinstance(shift, int):
        shift = shift % LANES
        return x if shift == 0 else pltpu.roll(x, shift, 1)
    return pltpu.roll(x, lax.rem(shift + 4 * LANES, LANES), 1)


def in_lanes(lane, start, width):
    return (lane >= start) & (lane < start + width)


def pick_lanes(x, index):
    return jnp.take_along_axis(x, index, axis=1, mode="promise_in_bounds")


def ranks(dest, groups):
    n = dest.shape[1]
    mine = iota((groups, n), 0) == dest
    hot = jnp.where(mine, 1.0, 0.0)
    earlier = jnp.where(iota((n, n), 0) < iota((n, n), 1), 1.0, 0.0).astype(jnp.bfloat16)
    count = jnp.dot(hot.astype(jnp.bfloat16), earlier, preferred_element_type=jnp.float32)
    return jnp.sum(jnp.where(mine, count, 0.0), axis=0, keepdims=True).astype(jnp.int32)


def one_hot_rows(slot, size):
    return jnp.where(iota((size, slot.shape[1]), 0) == slot, 1.0, 0.0).astype(jnp.bfloat16)


def route(x, hot):
    rows = x.shape[0]
    high = x.astype(jnp.bfloat16)
    rest = x - high.astype(jnp.float32)
    middle = rest.astype(jnp.bfloat16)
    low = (rest - middle.astype(jnp.float32)).astype(jnp.bfloat16)
    out = None
    for part in (low, middle, high):
        y = lax.dot_general(part, hot, (((1,), (1,)), ((), ())), preferred_element_type=jnp.float32)
        out = y if out is None else out + y
    return out


class Sizes:
    def __init__(self, comp, lev, levels, tracer_levels):
        self.C, self.L = comp, lev
        self.levels = levels
        self.slab = levels // lev
        self.K = LANES // comp
        self.chunks = tracer_levels // SUB
        self.NL = tracer_levels
        self.strip_rows = -(-SUB * self.chunks // SLOTS) * SUB
        self.low_rows = -(-4 * self.chunks // SLOTS) * SUB
        first = 4 * self.chunks // SLOTS
        self.high_base = first * SLOTS
        self.high_at = first * SUB
        self.strips = 1 if lev == 2 else 2
        self.corner_rows = max(self.low_rows, self.strip_rows - self.high_at)
        self.halo_rows = 4 * self.NL + self.strips * self.corner_rows
        self.blocks = LANES // CAP
        self.sources = self.blocks * lev
        self.wide = levels // SUB
        self.surf_at = self.wide * self.K
        self.list_at = self.surf_at + 3 * CAP
        assert comp * CAP == lev * LANES and levels % SUB == 0
        assert self.list_at + self.K <= LANES


def pack_strip(z, ocean, source):
    lane = iota((SUB, LANES), 1)
    tiles = []
    for first in range(0, SUB * z.chunks, SLOTS):
        tile = jnp.zeros((SUB, LANES), jnp.float32)
        for at in range(min(SLOTS, SUB * z.chunks - first)):
            row, chunk = divmod(first + at, z.chunks)
            piece = ocean[pl.ds(chunk * 64 + row, SUB, stride=SUB), :]
            piece = lane_roll(piece, at * STRIP - source)
            tile = jnp.where(in_lanes(lane, at * STRIP, STRIP), piece, tile)
        tiles.append(tile)
    return tiles


def select_kernel(z, temp, vapor, dest, owner, ocean, *outs):
    lev = lax.axis_index("lev")
    aux = outs[-1]
    d = dest[...]
    rank = ranks(d, z.C)
    slot = (rank // z.K) * LANES + d * z.K + lax.rem(rank, z.K)
    hot = one_hot_rows(slot, z.L * LANES)
    t_all = route(temp[...], hot)
    v_all = route(vapor[...], hot)
    if z.L == 2:
        keep, send = outs[0], outs[1]
        first = lev == 0
        for at, val in ((0, t_all), (z.slab, v_all)):
            a, b = val[:, :LANES], val[:, LANES:]
            keep[pl.ds(at, z.slab), :] = jnp.where(first, a, b)
            send[pl.ds(at, z.slab), :] = jnp.where(first, b, a)
        source = jnp.where(first, LANES - STRIP, 0)
        for i, tile in enumerate(pack_strip(z, ocean, source)):
            send[pl.ds(2 * z.slab + i * SUB, SUB), :] = tile
    else:
        slabs, right, left = outs[0], outs[1], outs[2]
        for h in range(z.L):
            slabs[h, : z.slab, :] = t_all[:, h * LANES : (h + 1) * LANES]
            slabs[h, z.slab :, :] = v_all[:, h * LANES : (h + 1) * LANES]
        for ref, source in ((right, LANES - STRIP), (left, 0)):
            for i, tile in enumerate(pack_strip(z, ocean, source)):
                ref[pl.ds(i * SUB, SUB), :] = tile
    o = owner[...]
    rank = ranks(o, z.C)
    hot = one_hot_rows(o * z.K + rank, LANES)
    number = iota((SUB, LANES), 1).astype(jnp.float32).astype(jnp.bfloat16)
    back = lax.dot_general(
        number, hot, (((1,), (1,)), ((), ())), preferred_element_type=jnp.float32
    )
    aux[:SUB, :] = back
    aux[SUB:, :] = jnp.broadcast_to(rank.astype(jnp.float32), (SUB, LANES))


def longwave(z, temp, vapor, kabs, pfrac, planck_s, vapor_s, kabs_s, pf_s, absorb_s, acc_s):
    levels, points = z.levels, kabs.shape[0]
    planck_s[...] = (temp * temp) * (temp * temp)
    vapor_s[...] = vapor * (-1.0 / math.log(2.0))
    kabs_s[:, : kabs.shape[1]] = kabs[...]
    pf_s[...] = jnp.broadcast_to(pfrac[...], (LANES, points)).T
    group = 8 * SUB
    width = group // SUB
    total = jnp.zeros((SUB, LANES), jnp.float32)
    for g0 in range(0, points, group):
        pf = [pf_s[pl.ds(g0 + i * SUB, SUB), :] for i in range(width)]

        def down_block(b, state):
            state = list(state)
            k0 = b * SUB
            kb = [
                lane_roll(kabs_s[pl.ds(g0 + i * SUB, SUB), :], LANES - k0) for i in range(width)
            ]
            for j in range(SUB):
                k = k0 + j
                vap = jnp.broadcast_to(vapor_s[pl.ds(k, 1), :], (SUB, LANES))
                pk = jnp.broadcast_to(planck_s[pl.ds(k, 1), :], (SUB, LANES))
                acc = None
                for i in range(width):
                    kk = jnp.broadcast_to(kb[i][:, j : j + 1], (SUB, LANES))
                    a = 1.0 - jnp.exp2(kk * vap)
                    absorb_s[pl.ds(k * points + g0 + i * SUB, SUB), :] = a
                    step = a * (pf[i] * pk - state[i])
                    state[i] = state[i] + step
                    acc = step if acc is None else acc + step
                at = pl.ds(k * SUB, SUB)
                if g0 == 0:
                    acc_s[at, :] = acc
                else:
                    acc_s[at, :] = acc_s[at, :] + acc
            return tuple(state)

        zero = jnp.zeros((SUB, LANES), jnp.float32)
        state = lax.fori_loop(0, levels // SUB, down_block, (zero,) * width)
        for part in state:
            total = total + part

        def up_block(step_b, state):
            state = list(state)
            k0 = (levels // SUB - 1 - step_b) * SUB
            for j in reversed(range(SUB)):
                k = k0 + j
                pk = jnp.broadcast_to(planck_s[pl.ds(k, 1), :], (SUB, LANES))
                acc = None
                for i in range(width):
                    a = absorb_s[pl.ds(k * points + g0 + i * SUB, SUB), :]
                    step = a * (pf[i] * pk - state[i])
                    state[i] = state[i] + step
                    acc = step if acc is None else acc + step
                at = pl.ds(k * SUB, SUB)
                acc_s[at, :] = acc_s[at, :] + acc
            return tuple(state)

        ground = jnp.broadcast_to(planck_s[pl.ds(levels - 1, 1), :], (SUB, LANES))
        lax.fori_loop(0, levels // SUB, up_block, tuple(p * ground for p in pf))
    warming = []
    for i in range(levels // SUB):
        w = None
        for s in range(SUB):
            part = acc_s[pl.ds(i * SUB * SUB + s, SUB, stride=SUB), :]
            w = part if w is None else w + part
        warming.append(w * (-1.0 / points))
    return warming, jnp.sum(total, axis=0, keepdims=True) * (1.0 / points)


def radiate_kernel(z, n_in, *refs):
    ins, outs, scratch = refs[:n_in], refs[n_in : n_in + 3], refs[n_in + 3 :]
    kabs, pfrac, aux, ocean = ins[:4]
    msg, north, south = outs
    lev = lax.axis_index("lev")
    temp_s, vap_s = scratch[0], scratch[1]
    if z.L == 2:
        keep, got = ins[4:]
        for at, ref in ((0, temp_s), (z.slab, vap_s)):
            a, b = keep[pl.ds(at, z.slab), :], got[pl.ds(at, z.slab), :]
            ref[: z.slab, :] = jnp.where(lev == 0, a, b)
            ref[z.slab :, :] = jnp.where(lev == 0, b, a)
        strips = [(got, 2 * z.slab)]
    else:
        slabs, from_left, from_right = ins[4:]
        for h in range(z.L):
            temp_s[h * z.slab : (h + 1) * z.slab, :] = slabs[h, : z.slab, :]
            vap_s[h * z.slab : (h + 1) * z.slab, :] = slabs[h, z.slab :, :]
        strips = [(from_left, 0), (from_right, 0)]
    for row in range(SUB):
        ref, q = (north, row) if row < 4 else (south, row - 4)
        for chunk in range(z.chunks):
            ref[pl.ds(q * z.NL + chunk * SUB, SUB), :] = ocean[
                pl.ds(chunk * 64 + row, SUB, stride=SUB), :
            ]
    for n, (ref, base) in enumerate(strips):
        at = 4 * z.NL + n * z.corner_rows
        rows = z.low_rows
        north[pl.ds(at, rows), :] = ref[pl.ds(base, rows), :]
        rows = z.strip_rows - z.high_at
        south[pl.ds(at, rows), :] = ref[pl.ds(base + z.high_at, rows), :]

    temp, vapor = temp_s[...], vap_s[...]
    warming, down = longwave(z, temp, vapor, kabs, pfrac, *scratch[2:])
    lane, sub = iota((SUB, LANES), 1), iota((SUB, LANES), 0)
    base = jnp.zeros((SUB, LANES), jnp.float32)
    surface = (down, temp_s[z.levels - 1 :, :], vap_s[z.levels - 1 :, :])
    for f, row in enumerate(surface):
        wide = jnp.broadcast_to(row, (SUB, LANES))
        at = z.surf_at + CAP * f
        for g in range(SUB):
            there = (sub == g) & in_lanes(lane, at, CAP)
            base = jnp.where(there, lane_roll(wide, at - CAP * g), base)
    back = aux[:SUB, :]
    for d in range(z.C):
        tile = jnp.where(
            in_lanes(lane, z.list_at, z.K), lane_roll(back, z.list_at - d * z.K), base
        )
        for i in range(z.wide):
            moved = lane_roll(warming[i], (i - d) * z.K)
            tile = jnp.where(in_lanes(lane, i * z.K, z.K), moved, tile)
        for h in range(z.L):
            msg[pl.ds((d * z.L + h) * SUB, SUB), :] = tile


class Halo:
    def __init__(self, z, from_north, from_south, strips):
        self.z, self.up, self.down, self.strips = z, from_north, from_south, strips
        lev, comp = lax.axis_index("lev"), lax.axis_index("comp")
        self.lane = iota((SUB, LANES), 1)
        if z.L == 2:
            self.targets = [jnp.where(lev == 0, 0, LANES - STRIP)]
        else:
            self.targets = [LANES - STRIP, 0]
        self.spots = [in_lanes(self.lane, t, STRIP) for t in self.targets]
        half = LANES // 2
        self.inside = ((self.lane < half) & (lev < z.L - 1)) | ((self.lane >= half) & (lev > 0))
        self.has_north = comp > 0
        self.has_south = comp < z.C - 1

    def edge(self, pieces, slot):
        out = jnp.zeros((SUB, LANES), jnp.float32)
        tile, place = lax.div(slot, SLOTS), lax.rem(slot, SLOTS) * STRIP
        for (ref, base), target, spot in zip(pieces, self.targets, self.spots):
            x = ref[pl.ds(pl.multiple_of(base + tile * SUB, SUB), SUB), :]
            out = jnp.where(spot, lane_roll(x, target - place), out)
        return out

    def chunk(self, i, own):
        z = self.z
        a, e = [], []
        corners = [4 * z.NL + n * z.corner_rows for n in range(z.strips)]
        for q in range(4):
            a.append(self.up[pl.ds(pl.multiple_of(q * z.NL + i * SUB, SUB), SUB), :])
            slot = (4 + q) * z.chunks - z.high_base + i
            e.append(self.edge([(self.up, c) for c in corners], slot))
        for r in range(SUB):
            a.append(own(r))
            e.append(self.edge(self.strips, r * z.chunks + i))
        for q in range(4):
            a.append(self.down[pl.ds(pl.multiple_of(q * z.NL + i * SUB, SUB), SUB), :])
            e.append(self.edge([(self.down, c) for c in corners], q * z.chunks + i))
        rows = 16
        first, last = self.lane == 0, self.lane == LANES - 1
        for step in range(NSTEP):
            na, ne = [None] * rows, [None] * rows
            for y in range(step + 1, rows - 1 - step):
                al, el = lane_roll(a[y], 1), lane_roll(e[y], 1)
                ar, er = lane_roll(a[y], LANES - 1), lane_roll(e[y], LANES - 1)

                def stepped(x, up, down, left, right):
                    beside = (up + down) + (left + right)
                    return (1.0 - 4.0 * diffusion_rate) * x + diffusion_rate * beside

                na[y] = stepped(
                    a[y], a[y - 1], a[y + 1], jnp.where(first, el, al), jnp.where(last, er, ar)
                )
                if y < 4:
                    na[y] = jnp.where(self.has_north, na[y], 0.0)
                elif y >= 12:
                    na[y] = jnp.where(self.has_south, na[y], 0.0)
                if step < NSTEP - 1:
                    keep = self.inside
                    if y < 4:
                        keep = keep & self.has_north
                    elif y >= 12:
                        keep = keep & self.has_south
                    side = stepped(
                        e[y], e[y - 1], e[y + 1], jnp.where(first, al, el), jnp.where(last, ar, er)
                    )
                    ne[y] = jnp.where(keep, side, 0.0)
            a, e = na, ne
        return a[4:12]


def halo_of(z, refs):
    if z.L == 2:
        return Halo(z, refs[0], refs[1], [(refs[2], 2 * z.slab)])
    return Halo(z, refs[0], refs[1], [(refs[2], 0), (refs[3], 0)])


def surface_kernel(z, got, idx, weight, gust, pos, share, theta, salt, *refs):
    halo = halo_of(z, refs[:-2])
    top, out = refs[-2:]
    lev = lax.axis_index("lev")
    lane, sub = iota((SUB, LANES), 1), iota((SUB, LANES), 0)
    for n, ref in enumerate((theta, salt)):
        rows = halo.chunk(
            jnp.int32(n * (z.chunks // 2)), lambda r: ref[pl.ds(r, SUB, stride=SUB), :]
        )
        for r in range(SUB):
            top[pl.ds(n * 64 + r, SUB, stride=SUB), :] = rows[r]
    p = jnp.zeros((SUB, LANES), jnp.float32)
    for b in range(z.C):
        x = got[pl.ds(pl.multiple_of((b * z.L + lev) * SUB, SUB), SUB), :]
        p = jnp.where(in_lanes(lane, b * z.K, z.K), lane_roll(x, b * z.K - z.list_at), p)
    p = p.astype(jnp.int32)
    source = p // z.K
    slot = (lane // z.K) * z.K + lax.rem(p, z.K)
    place = lax.rem(slot, CAP) + z.surf_at
    row_ok = (slot // CAP) == sub
    parts = [jnp.zeros((SUB, LANES), jnp.float32)] * 3
    for s in range(z.sources):
        x = got[pl.ds(pl.multiple_of((lev * z.sources + s) * SUB, SUB), SUB), :]
        there = row_ok & (source == s)
        for f in range(3):
            parts[f] = jnp.where(there, pick_lanes(x, place + CAP * f), parts[f])
    intake = [
        jnp.broadcast_to(jnp.sum(v, axis=0, keepdims=True), (SUB, LANES)) for v in parts
    ]
    fields = [None] * 3
    for m in range(idx.shape[0] // SUB):
        at = idx[pl.ds(m * SUB, SUB), :]
        w = weight[pl.ds(m * SUB, SUB), :]
        for f in range(3):
            term = w * pick_lanes(intake[f], at)
            fields[f] = term if m == 0 else fields[f] + term
    th, sa = top[:SUB, :], top[64 : 64 + SUB, :]
    wind = gust[...]
    sst = 1.0 + th
    square = sst * sst
    heat = (
        fields[0]
        - skin_radiative_efficiency * (square * square)
        + thermal_coupling_coefficient * wind * (fields[1] - sst)
    )
    humid = clausius_magnitude * jnp.exp(clausius_gradient * (sst - 1.0))
    evap = evap_coef * wind * (humid - fields[2])
    th_new = th + thermal_increment * heat
    top[:SUB, :] = th_new
    top[64 : 64 + SUB, :] = sa + salt_step * (1.0 + sa) * evap
    sst_new = 1.0 + th_new
    total = jnp.zeros((SUB, LANES), jnp.float32)
    for m in range(pos.shape[0]):
        cell = jnp.broadcast_to(pos[pl.ds(m, 1), :], (SUB, LANES))
        picked = pick_lanes(sst_new, cell & (LANES - 1))
        hit = jnp.where((cell // LANES) == sub, picked, 0.0)
        total = total + hit * jnp.broadcast_to(share[pl.ds(m, 1), :], (SUB, LANES))
    slot_sst = jnp.sum(total, axis=0, keepdims=True)
    out[...] = jnp.broadcast_to(slot_sst, out.shape)


def diffuse_kernel(z, ocean, got, top, *refs):
    halo = halo_of(z, refs[:-2])
    marine, warm = refs[-2:]
    lev = lax.axis_index("lev")
    lane = iota((SUB, LANES), 1)
    half = z.chunks // 2

    def one(i, carry):
        base = pl.multiple_of(i * 64, 64)
        rows = halo.chunk(i, lambda r: ocean[pl.ds(base + r, SUB, stride=SUB), :])
        for r in range(SUB):
            marine[pl.ds(base + r, SUB, stride=SUB), :] = rows[r]
        return carry

    for n in range(2):
        marine[pl.ds(n * half * 64, 64), :] = top[pl.ds(n * 64, 64), :]
        lax.fori_loop(n * half + 1, (n + 1) * half, one, 0)
    tiles = [jnp.zeros((SUB, LANES), jnp.float32)] * z.wide
    for s in range(z.sources):
        x = got[pl.ds(pl.multiple_of((lev * z.sources + s) * SUB, SUB), SUB), :]
        spot = in_lanes(lane, s * z.K, z.K)
        for i in range(z.wide):
            tiles[i] = jnp.where(spot, lane_roll(x, (s - i) * z.K), tiles[i])
    for i in range(z.wide):
        warm[pl.ds(i * SUB, SUB), :] = tiles[i]


def place_kernel(z, got, owner, aux, out):
    comp = lax.axis_index("comp")
    rank = aux[SUB : SUB + 1, :].astype(jnp.int32)
    own = owner[...]
    index = jnp.broadcast_to(comp * z.K + rank, (z.C, LANES))
    picked = pick_lanes(got[...], index)
    hit = jnp.where(iota((z.C, LANES), 0) == own, picked, 0.0)
    out[...] = jnp.sum(hit, axis=0, keepdims=True)


def f32(*shape):
    return jax.ShapeDtypeStruct(shape, jnp.float32)


def call(body, z, args, out_shape, name, scratch=(), specs=None):
    single = not isinstance(out_shape, (list, tuple))
    return pl.pallas_call(
        lambda *refs: body(z, *refs),
        out_shape=out_shape,
        in_specs=specs or [VMEM] * len(args),
        out_specs=VMEM if single else [VMEM] * len(out_shape),
        scratch_shapes=list(scratch),
        name=name,
    )(*args)


def local(
    atm_temp,
    atm_vapor,
    span_dest,
    kabs,
    pfrac,
    ocean_owner,
    remap_idx,
    remap_w,
    gust,
    ocean_state,
    gather_positions,
    gather_shares,
):
    comp, lev = lax.axis_size("comp"), lax.axis_size("lev")
    tracers, depth, rows, cols = ocean_state.shape
    assert rows == SUB and cols == LANES and tracers == 2
    z = Sizes(comp, lev, atm_temp.shape[0] * lev, tracers * depth)
    ocean = ocean_state.reshape(z.NL * SUB, LANES)
    dest = span_dest.reshape(1, -1)
    owner = ocean_owner.reshape(1, -1)
    strip = f32(z.strip_rows, LANES)
    args = (atm_temp, atm_vapor, dest, owner, ocean)
    aux_shape = f32(2 * SUB, LANES)
    if lev == 2:
        half = 2 * z.slab
        keep, send, aux = call(
            select_kernel,
            z,
            args,
            [f32(half, LANES), f32(half + z.strip_rows, LANES), aux_shape],
            "select",
        )
        got = lax.ppermute(send, "lev", [(0, 1), (1, 0)])
        state = (keep, got)
        strips = (got,)
    else:
        slabs, right, left, aux = call(
            select_kernel, z, args, [f32(lev, 2 * z.slab, LANES), strip, strip, aux_shape], "select"
        )
        slabs = lax.all_to_all(slabs, "lev", split_axis=0, concat_axis=0, tiled=True)
        up = [(i, i + 1) for i in range(lev - 1)]
        from_left = lax.ppermute(right, "lev", up)
        from_right = lax.ppermute(left, "lev", [(j, i) for i, j in up])
        state = (slabs, from_left, from_right)
        strips = (from_left, from_right)
    points = kabs.shape[0]
    table = f32(z.levels, LANES)
    halo = f32(z.halo_rows, LANES)
    args = (kabs, pfrac.reshape(1, -1), aux, ocean) + state
    msg, north, south = call(
        lambda z, *refs: radiate_kernel(z, len(args), *refs),
        z,
        args,
        [f32(comp * lev * SUB, LANES), halo, halo],
        "radiate",
        [
            pltpu.VMEM((z.levels, LANES), jnp.float32),
            pltpu.VMEM((z.levels, LANES), jnp.float32),
            pltpu.VMEM((z.levels, LANES), jnp.float32),
            pltpu.VMEM((z.levels, LANES), jnp.float32),
            pltpu.VMEM((points, LANES), jnp.float32),
            pltpu.VMEM((points, LANES), jnp.float32),
            pltpu.VMEM((z.levels * points, LANES), jnp.float32),
            pltpu.VMEM((z.levels * SUB, LANES), jnp.float32),
        ],
    )
    msgs = lax.all_to_all(
        msg.reshape(comp * lev, SUB, LANES), ("comp", "lev"), split_axis=0, concat_axis=0, tiled=True
    ).reshape(comp * lev * SUB, LANES)
    up = [(i, i + 1) for i in range(comp - 1)]
    from_north = lax.ppermute(south, "comp", up)
    from_south = lax.ppermute(north, "comp", [(j, i) for i, j in up])
    halos = (from_north, from_south) + strips
    taps = remap_idx.shape[0]
    block = z.chunks // 2 * 64
    top, slots = call(
        surface_kernel,
        z,
        (
            msgs,
            remap_idx.reshape(taps * SUB, LANES),
            remap_w.reshape(taps * SUB, LANES),
            gust,
            gather_positions,
            gather_shares,
            lax.slice_in_dim(ocean, 0, 64, axis=0),
            lax.slice_in_dim(ocean, block, block + 64, axis=0),
        )
        + halos,
        [f32(128, LANES), f32(comp, LANES)],
        "surface",
    )
    back = lax.all_to_all(slots, "comp", split_axis=0, concat_axis=0, tiled=True)
    marine, warm = call(
        diffuse_kernel,
        z,
        (ocean, msgs, top) + halos,
        [f32(z.NL * SUB, LANES), f32(z.levels, LANES)],
        "diffuse",
    )
    skin = call(place_kernel, z, (back, owner, aux), f32(1, LANES), "place")
    return warm, marine.reshape(ocean_state.shape), skin.reshape(-1)


def solution(mesh):
    in_specs = (
        P("lev", "comp"),
        P("lev", "comp"),
        P("comp"),
        P(),
        P(),
        P(("comp", "lev")),
        P(None, "comp", "lev"),
        P(None, "comp", "lev"),
        P("comp", "lev"),
        P(None, None, "comp", "lev"),
        P(None, ("comp", "lev")),
        P(None, ("comp", "lev")),
    )
    out_specs = (P(None, ("comp", "lev")), P(None, None, "comp", "lev"), P(("comp", "lev")))
    return jax.shard_map(local, mesh=mesh, in_specs=in_specs, out_specs=out_specs, check_vma=False)
```
